512 devices in a mesh: ep: 128 (over z, y, core), tp: 4 (over x).
Axes of the slice: x: 4, y: 4, z: 16, core: 2. Of those that a mesh axis runs over, the one named last changes fastest.
Arguments:
- tokens: bfloat16 [16384, 2048], P('ep', 'tp'), may hold values from -6 to 6
- cotangent: bfloat16 [16384, 2048], P('ep', 'tp'), may hold values from -6 to 6
- token_expert: int32 [16384], P('ep'), may hold values from 0 to 127, as said below
- partner: int32 [128], replicated, may hold values from 0 to 127, as said below
- gate_weight: bfloat16 [128, 768, 2048], P('ep', 'tp'), may hold values from -0.125 to 0.125
- up_weight: bfloat16 [128, 768, 2048], P('ep', 'tp'), may hold values from -0.125 to 0.125
- down_weight: bfloat16 [128, 768, 2048], P('ep', 'tp'), may hold values from -0.21875 to 0.21875
Outputs:
- token_grad: bfloat16 [16384, 2048], P('ep', 'tp')
- gate_grad: bfloat16 [128, 768, 2048], P('ep', 'tp')
- up_grad: bfloat16 [128, 768, 2048], P('ep', 'tp')
- down_grad: bfloat16 [128, 768, 2048], P('ep', 'tp')
The draws below stay inside these ranges and needn't reach their ends.
Inputs may be any that keep to these rules, and one draw needn't show every extreme that they name: partner[partner[d]] = d and partner[d] != d: the devices of ep swap their experts in pairs. `token_expert`: each aligned block of 128 rows (the rows of one device) names each expert at most 2 times, and one expert, the same for all blocks, exactly 2 times in every block.
All inputs are finite; a program needn't handle non-finite values.
Results may differ from the reference program's by a relative error of at most 0.0049.
Values may be sent and summed in bfloat16 or wider, within the bound.
No kernel may reach another device: no remote copies, remote signals or barrier semaphores. Data moves between devices by JAX's collectives and lax.ppermute only.
A program may use at most 64 MiB of HBM per device.

```python
import jax
import jax.numpy as jnp
from jax import lax

D = 2048
F = 768
TOK_DEV = 128
EXPERTS = 128
CAP = 2
ROWS = 16384
N_EP = 128


def draw_partner(key, part):
    shuffled = jax.random.permutation(key, EXPERTS).astype(jnp.int32)
    paired = shuffled.reshape(-1, 2)[:, ::-1].reshape(-1)
    return jnp.zeros((EXPERTS,), jnp.int32).at[shuffled].set(paired)


def draw_token_expert(key, part):
    hottest = jax.random.randint(jax.random.fold_in(key, 7), (), 0, EXPERTS).astype(jnp.int32)

    def one_block(block_index):
        sub_key = jax.random.fold_in(key, block_index)
        scores = jax.random.permutation(jax.random.fold_in(sub_key, 1), EXPERTS * CAP).astype(jnp.int32)
        slot_ids = jnp.arange(EXPERTS * CAP, dtype=jnp.int32)
        owners = slot_ids // CAP
        scores = jnp.where(owners == hottest, slot_ids % CAP - CAP, scores)
        chosen = owners[jnp.argsort(scores, stable=True)][:TOK_DEV]
        return chosen[jax.random.permutation(jax.random.fold_in(sub_key, 2), TOK_DEV)]
    return jax.vmap(one_block)(jnp.arange(N_EP, dtype=jnp.int32)).reshape(-1).astype(jnp.int32)


def block_scale(key, extent, pieces, low, largest):
    loudness, own = 1.0, jax.random.fold_in(key, 6)
    for dim, shards_of in pieces:
        draws = jnp.exp(jax.random.uniform(jax.random.fold_in(own, dim), (shards_of,), jnp.float32, low / len(pieces), largest / len(pieces)))
        loudness = loudness * jnp.repeat(draws, extent[dim] // shards_of).reshape([-1 if axis == dim else 1 for axis in range(len(extent))])
    return loudness


def gaussian(stream_key, shape, scale, reach, split=(), kind=jnp.bfloat16):
    array = jax.random.normal(stream_key, shape, jnp.float32) * scale
    if len(split) > 0:
        array = block_scale(stream_key, shape, split, -0.22, 0.18) * array
    return jnp.clip(array, min=-reach, max=reach).astype(kind)


def setup_inputs(seed: int = 0) -> dict:
    arg_keys = jax.random.split(jax.random.key(seed), 8)
    tokens = gaussian(arg_keys[0], (ROWS, D), 1.0, 6.0, ((0, 128), (1, 4)))
    cotangent = gaussian(arg_keys[1], (ROWS, D), 1.0, 6.0, ((0, 128), (1, 4)))
    token_expert = draw_token_expert(jax.random.fold_in(arg_keys[7], 71), 0)
    partner = draw_partner(jax.random.fold_in(arg_keys[7], 71), 0)
    gate_weight = gaussian(arg_keys[4], (EXPERTS, F, D), D ** -0.5, 0.125, ((0, 128), (1, 4)))
    up_weight = gaussian(arg_keys[5], (EXPERTS, F, D), D ** -0.5, 0.125, ((0, 128), (1, 4)))
    down_weight = gaussian(arg_keys[6], (EXPERTS, F, D), F ** -0.5, 0.21875, ((0, 128), (1, 4)))
    return dict(tokens=tokens, cotangent=cotangent, token_expert=token_expert, partner=partner, gate_weight=gate_weight, up_weight=up_weight, down_weight=down_weight)


def expert_math(full_x, full_g, w_gate, w_up, w_down):
    gate = jnp.dot(full_x, w_gate.T, preferred_element_type=jnp.float32)
    upward = jnp.dot(full_x, w_up.T, preferred_element_type=jnp.float32)
    sigmoid_gate = jax.nn.sigmoid(gate)
    activated = gate * sigmoid_gate
    hidden = (activated * upward).astype(jnp.bfloat16)
    hidden_grad = jnp.dot(full_g, w_down.T, preferred_element_type=jnp.float32)
    up_term = (hidden_grad * activated).astype(jnp.bfloat16)
    gate_term = (hidden_grad * upward * sigmoid_gate * (1.0 + gate * (1.0 - sigmoid_gate))).astype(jnp.bfloat16)
    row_grad = jnp.dot(gate_term, w_gate, preferred_element_type=jnp.float32) + jnp.dot(up_term, w_up, preferred_element_type=jnp.float32)
    grad_gate = jnp.dot(gate_term.T, full_x, preferred_element_type=jnp.float32).astype(jnp.bfloat16)
    grad_up = jnp.dot(up_term.T, full_x, preferred_element_type=jnp.float32).astype(jnp.bfloat16)
    grad_down = jnp.dot(hidden.T, full_g, preferred_element_type=jnp.float32).astype(jnp.bfloat16)
    return row_grad.astype(jnp.bfloat16), grad_gate, grad_up, grad_down


def reference(tokens, cotangent, token_expert, partner, gate_weight, up_weight, down_weight):
    capacity = N_EP * CAP
    row_total = tokens.shape[0]
    owners = token_expert.astype(jnp.int32)
    sorted_rows = jnp.argsort(owners, stable=True).astype(jnp.int32)
    counts = jnp.sum((owners[None, :] == jnp.arange(EXPERTS, dtype=jnp.int32)[:, None]).astype(jnp.int32), axis=1)
    starts = (jnp.cumsum(counts) - counts).astype(jnp.int32)
    offsets = jnp.arange(capacity, dtype=jnp.int32)
    picked = jnp.take(sorted_rows, jnp.minimum(starts[:, None] + offsets[None, :], row_total - 1))
    picked = jnp.where(offsets[None, :] < counts[:, None], picked, row_total).astype(jnp.int32)
    padded_x = jnp.concatenate([tokens, jnp.zeros((1, D), jnp.bfloat16)], axis=0)
    padded_g = jnp.concatenate([cotangent, jnp.zeros((1, D), jnp.bfloat16)], axis=0)

    def expert_step(inputs):
        rows_of, w_gate, w_up, w_down = inputs
        return expert_math(padded_x[rows_of], padded_g[rows_of], w_gate, w_up, w_down)

    row_grads, grad_gate, grad_up, grad_down = lax.map(expert_step, (picked, gate_weight, up_weight, down_weight))
    token_grad = jnp.zeros((row_total + 1, D), jnp.bfloat16).at[picked.reshape(-1)].set(row_grads.reshape(-1, D))[:row_total]
    gate_grad = jnp.take(grad_gate, partner.astype(jnp.int32), axis=0)
    up_grad = jnp.take(grad_up, partner.astype(jnp.int32), axis=0)
    down_grad = jnp.take(grad_down, partner.astype(jnp.int32), axis=0)
    return token_grad, gate_grad, up_grad, down_grad
```

```python
import jax
import jax.numpy as jnp
from jax import lax
from jax.sharding import PartitionSpec as P


def contract_last(left, right):
    return lax.dot_general(
        left, right, (((1,), (1,)), ((), ())), preferred_element_type=jnp.float32
    )


def contract_first(left, right):
    return lax.dot_general(
        left, right, (((0,), (0,)), ((), ())), preferred_element_type=jnp.float32
    )


def exchange(array):
    devices = lax.axis_size("ep")
    rows, width = array.shape
    parts = array.reshape(devices, rows // devices, width)
    parts = lax.all_to_all(parts, "ep", split_axis=0, concat_axis=0, tiled=True)
    return parts.reshape(rows, width)


def all_features(received, width):
    stacked = jnp.concatenate([received[:, :width], received[:, width:]], axis=0)
    full = lax.all_gather(stacked, "tp", axis=1, tiled=True)
    slots = received.shape[0]
    return full[:slots], full[slots:]


def body(tokens, cotangent, token_expert, partner, gate_weight, up_weight, down_weight):
    devices = lax.axis_size("ep")
    row_count, width = tokens.shape
    capacity = max(2, (2 * row_count + devices - 1) // devices)
    slots = devices * capacity
    w_gate = gate_weight[0]
    w_up = up_weight[0]
    w_down = down_weight[0]
    hidden_count = w_gate.shape[0]

    same_expert = token_expert[:, None] == token_expert[None, :]
    earlier = jnp.arange(row_count)[:, None] > jnp.arange(row_count)[None, :]
    position = jnp.sum((same_expert & earlier).astype(jnp.int32), axis=1)
    slot_of = token_expert * capacity + position
    new_slot_of = partner.at[token_expert].get(mode="promise_in_bounds") * capacity + position
    slot_ids = jnp.arange(slots)[:, None]
    one_hot = (slot_of[None, :] == slot_ids).astype(jnp.bfloat16)
    new_one_hot = (new_slot_of[None, :] == slot_ids).astype(jnp.bfloat16)
    both = jnp.concatenate([tokens, cotangent], axis=1)
    send_old = jnp.dot(one_hot, both, preferred_element_type=jnp.float32).astype(jnp.bfloat16)
    send_new = jnp.dot(new_one_hot, both, preferred_element_type=jnp.float32).astype(jnp.bfloat16)

    received = exchange(send_old)
    send_new, received = lax.optimization_barrier((send_new, received))
    received_new = exchange(send_new)
    full_x, full_g = all_features(received, width)

    gate = contract_last(full_x, w_gate)
    upward = contract_last(full_x, w_up)
    sigmoid_gate = jax.nn.sigmoid(gate)
    activated = gate * sigmoid_gate
    hidden = (activated * upward).astype(jnp.bfloat16)
    hidden_grad = contract_last(full_g, w_down)
    up_term = (hidden_grad * activated).astype(jnp.bfloat16)
    gate_term = (
        hidden_grad * upward * sigmoid_gate * (1.0 + gate * (1.0 - sigmoid_gate))
    ).astype(jnp.bfloat16)
    partial_value = (
        jnp.dot(gate_term, w_gate, preferred_element_type=jnp.float32)
        + jnp.dot(up_term, w_up, preferred_element_type=jnp.float32)
    ).astype(jnp.bfloat16)
    terms = jnp.concatenate([gate_term, up_term, hidden], axis=1)

    share = lax.psum_scatter(partial_value, "tp", scatter_dimension=1, tiled=True)
    at_source = exchange(terms)
    onward = at_source.reshape(devices, capacity, -1).at[partner].get(mode="promise_in_bounds")
    onward = onward.reshape(slots, 3 * hidden_count)
    share, received_new = lax.optimization_barrier((share, received_new))
    new_x, new_g = all_features(received_new, width)
    arrived = exchange(jnp.concatenate([share, onward], axis=1))
    coming_back = arrived[:, :width]
    terms = arrived[:, width:]
    token_grad = contract_first(one_hot, coming_back).astype(jnp.bfloat16)
    gate_term = terms[:, :hidden_count]
    up_term = terms[:, hidden_count : 2 * hidden_count]
    hidden = terms[:, 2 * hidden_count :]
    grad_gate = contract_first(gate_term, new_x).astype(jnp.bfloat16)[None]
    grad_up = contract_first(up_term, new_x).astype(jnp.bfloat16)[None]
    grad_down = contract_first(hidden, new_g).astype(jnp.bfloat16)[None]
    return (token_grad, grad_gate, grad_up, grad_down)


def solution(mesh):
    in_specs = (
        P("ep", "tp"),
        P("ep", "tp"),
        P("ep"),
        P(),
        P("ep", "tp", None),
        P("ep", "tp", None),
        P("ep", "tp", None),
    )
    out_specs = (P("ep", "tp"), P("ep", "tp", None), P("ep", "tp", None), P("ep", "tp", None))
    return jax.shard_map(body, mesh=mesh, in_specs=in_specs, out_specs=out_specs, check_vma=False)
```

```python
import jax
import jax.numpy as jnp
from jax import lax
from jax.experimental import pallas as pl
from jax.experimental.pallas import tpu as pltpu
from jax.sharding import PartitionSpec as P


ROWS_WITH_ROWS = (((0,), (0,)), ((), ()))
LAST_WITH_LAST = (((1,), (1,)), ((), ()))


def dot(left, right, dims=(((1,), (0,)), ((), ()))):
    return lax.dot_general(left, right, dims, preferred_element_type=jnp.float32)


def by_owner(array):
    devices = lax.axis_size("ep")
    return array.reshape(devices, array.shape[0] // devices, array.shape[1])


def by_slot(parts):
    return parts.reshape(parts.shape[0] * parts.shape[1], parts.shape[2])


def exchange(parts):
    return lax.all_to_all(parts, "ep", split_axis=0, concat_axis=0, tiled=True)


def shifted(array, step):
    size = lax.axis_size("tp")
    return lax.ppermute(array, "tp", [(i, (i + step) % size) for i in range(size)])


def everyones(received, width):
    stacked = jnp.concatenate([received[:, :width], received[:, width:]], axis=0)
    steps = sorted(range(1, lax.axis_size("tp")), key=lambda k: k != 2)
    pieces = {0: stacked}
    for step in steps:
        pieces[step] = shifted(stacked, step)
    return [pieces[k] for k in range(len(pieces))]


def dispatch_kernel(expert_ref, tokens_ref, cotangent_ref, send_ref, slot_ref, *, capacity):
    count = tokens_ref.shape[0]
    width = tokens_ref.shape[1]
    slots = send_ref.shape[0]
    experts = jnp.broadcast_to(expert_ref[...], (count, count))
    same = experts == experts.T
    row = lax.broadcasted_iota(jnp.int32, (count, count), 0)
    column = lax.broadcasted_iota(jnp.int32, (count, count), 1)
    position = jnp.sum(jnp.where(same & (row < column), 1, 0), axis=0, keepdims=True)
    slot = expert_ref[...] * capacity + position
    slot_ref[...] = slot
    chosen = lax.broadcasted_iota(jnp.int32, (slots, count), 0) == slot
    one_hot = jnp.where(chosen, 1.0, 0.0).astype(jnp.bfloat16)
    send_ref[:, :width] = dot(one_hot, tokens_ref[...]).astype(jnp.bfloat16)
    send_ref[:, width:] = dot(one_hot, cotangent_ref[...]).astype(jnp.bfloat16)


def terms_kernel(place_ref, *refs, ways, slots, width):
    pieces, (gate_ref, up_ref, down_ref, terms_ref) = refs[:ways], refs[ways:]
    hidden_count = gate_ref.shape[0]
    gate = upward = hidden_grad = 0.0
    for step in range(ways):
        start = pl.multiple_of(lax.rem(place_ref[0] + ways - step, ways) * width, 128)
        features = pl.ds(start, width)
        x = pieces[step][:slots, :]
        g = pieces[step][slots:, :]
        gate = gate + dot(x, gate_ref[:, features], LAST_WITH_LAST)
        upward = upward + dot(x, up_ref[:, features], LAST_WITH_LAST)
        hidden_grad = hidden_grad + dot(g, down_ref[:, features], LAST_WITH_LAST)
    sigmoid_gate = jax.nn.sigmoid(gate)
    activated = gate * sigmoid_gate
    gate_term = hidden_grad * upward * sigmoid_gate * (1.0 + gate * (1.0 - sigmoid_gate))
    terms_ref[:, :hidden_count] = gate_term.astype(jnp.bfloat16)
    terms_ref[:, hidden_count : 2 * hidden_count] = (hidden_grad * activated).astype(jnp.bfloat16)
    terms_ref[:, 2 * hidden_count :] = (activated * upward).astype(jnp.bfloat16)


def partial_kernel(place_ref, terms_ref, gate_ref, up_ref, *outs, ways, width):
    hidden_count = gate_ref.shape[0]
    gate_term = terms_ref[:, :hidden_count]
    up_term = terms_ref[:, hidden_count : 2 * hidden_count]
    for step in range(ways):
        start = pl.multiple_of(lax.rem(place_ref[0] + step, ways) * width, 128)
        features = pl.ds(start, width)
        value = dot(gate_term, gate_ref[:, features]) + dot(up_term, up_ref[:, features])
        outs[step][...] = value.astype(outs[step].dtype)


def final_kernel(place_ref, slot_ref, arrived_ref, *refs, ways, slots, width, hidden_count):
    pieces, (token_ref, gate_ref, up_ref, down_ref) = refs[:ways], refs[ways:]
    step = pl.program_id(0)
    first = arrived_ref[:, width : width + hidden_count]
    second = arrived_ref[:, width + hidden_count : width + 2 * hidden_count]
    third = arrived_ref[:, width + 2 * hidden_count : width + 3 * hidden_count]
    for turn in range(ways):

        @pl.when(step == turn)
        def _(turn=turn):
            x = pieces[turn][:slots, :]
            g = pieces[turn][slots:, :]
            gate_ref[...] = dot(first, x, ROWS_WITH_ROWS).astype(jnp.bfloat16)
            up_ref[...] = dot(second, x, ROWS_WITH_ROWS).astype(jnp.bfloat16)
            down_ref[...] = dot(third, g, ROWS_WITH_ROWS).astype(jnp.bfloat16)
            if turn == 0:
                count = token_ref.shape[0]
                chosen = lax.broadcasted_iota(jnp.int32, (slots, count), 0) == slot_ref[...]
                one_hot = jnp.where(chosen, 1.0, 0.0).astype(jnp.bfloat16)
                back = dot(one_hot, arrived_ref[:, :width], ROWS_WITH_ROWS)
                token_ref[...] = back.astype(jnp.bfloat16)


def near(array):
    return pltpu.with_memory_space_constraint(array, pltpu.VMEM)


SMALL = pl.BlockSpec(memory_space=pltpu.SMEM)
WHOLE = pl.BlockSpec(memory_space=pltpu.VMEM)


def body(tokens, cotangent, token_expert, partner, gate_weight, up_weight, down_weight):
    devices = lax.axis_size("ep")
    ways = lax.axis_size("tp")
    row_count, width = tokens.shape
    capacity = max(2, (2 * row_count + devices - 1) // devices)
    slots = devices * capacity
    w_gate = gate_weight[0]
    w_up = up_weight[0]
    w_down = down_weight[0]
    hidden_count = w_gate.shape[0]
    place = lax.axis_index("tp").astype(jnp.int32).reshape(1)

    def shape(*dims, kind=jnp.bfloat16):
        return jax.ShapeDtypeStruct(dims, kind)

    send_old, slot_row = pl.pallas_call(
        lambda *refs: dispatch_kernel(*refs, capacity=capacity),
        out_shape=(pltpu.VMEM((slots, 2 * width), jnp.bfloat16), shape(1, row_count, kind=jnp.int32)),
        in_specs=[WHOLE] * 3,
        out_specs=(WHOLE, WHOLE),
        name="dispatch",
    )(token_expert.reshape(1, row_count), tokens, cotangent)
    received = exchange(by_owner(send_old))

    slot_of = slot_row[0]
    owners = partner.at[token_expert].get(mode="promise_in_bounds")
    new_slot_of = slot_of + (owners - token_expert) * capacity
    new_one_hot = (new_slot_of[None, :] == jnp.arange(slots)[:, None]).astype(jnp.bfloat16)
    both = jnp.concatenate([tokens, cotangent], axis=1)
    send_new = by_owner(dot(new_one_hot, both).astype(jnp.bfloat16))
    send_new, received = lax.optimization_barrier((send_new, received))
    received_new = exchange(send_new)
    pieces = everyones(by_slot(received), width)
    terms = pl.pallas_call(
        lambda *refs: terms_kernel(*refs, ways=ways, slots=slots, width=width),
        out_shape=pltpu.VMEM((slots, 3 * hidden_count), jnp.bfloat16),
        in_specs=[SMALL] + [WHOLE] * (ways + 3),
        out_specs=WHOLE,
        name="terms",
    )(place, *map(near, pieces), w_gate, w_up, w_down)
    sent, received_new = lax.optimization_barrier((by_owner(terms), received_new))
    at_source = exchange(sent)
    kinds = [jnp.float32] + [jnp.bfloat16] * (ways - 1)
    partials = pl.pallas_call(
        lambda *refs: partial_kernel(*refs, ways=ways, width=width),
        out_shape=tuple(pltpu.VMEM((slots, width), kind) for kind in kinds),
        in_specs=[SMALL] + [WHOLE] * 3,
        out_specs=(WHOLE,) * ways,
        name="partials",
    )(place, near(terms), w_gate, w_up)
    share = partials[0]
    for step in sorted(range(1, ways), key=lambda k: k != 2):
        share = share + shifted(partials[step], step).astype(jnp.float32)
    share = share.astype(jnp.bfloat16)
    onward = at_source.at[partner].get(mode="promise_in_bounds")
    share, received_new = lax.optimization_barrier((share, received_new))
    new_pieces = everyones(by_slot(received_new), width)
    arrived = by_slot(exchange(jnp.concatenate([by_owner(share), onward], axis=2)))
    turned = lambda step, place_ref: (0, lax.rem(place_ref[0] + ways - step, ways))
    fixed = lambda step, place_ref: (0, 0)
    part = pl.BlockSpec((hidden_count, width), turned)
    token_grad, grad_gate, grad_up, grad_down = pl.pallas_call(
        lambda *refs: final_kernel(
            *refs, ways=ways, slots=slots, width=width, hidden_count=hidden_count
        ),
        out_shape=(shape(row_count, width),) + (shape(hidden_count, ways * width),) * 3,
        grid_spec=pltpu.PrefetchScalarGridSpec(
            num_scalar_prefetch=1,
            grid=(ways,),
            in_specs=[WHOLE] * (2 + ways),
            out_specs=(pl.BlockSpec((row_count, width), fixed), part, part, part),
        ),
        name="final",
    )(place, slot_row, near(arrived), *map(near, new_pieces))
    return (token_grad, grad_gate[None], grad_up[None], grad_down[None])


def solution(mesh):
    in_specs = (
        P("ep", "tp"),
        P("ep", "tp"),
        P("ep"),
        P(),
        P("ep", "tp", None),
        P("ep", "tp", None),
        P("ep", "tp", None),
    )
    out_specs = (P("ep", "tp"), P("ep", "tp", None), P("ep", "tp", None), P("ep", "tp", None))
    return jax.shard_map(body, mesh=mesh, in_specs=in_specs, out_specs=out_specs, check_vma=False)
```
